32 devices in a mesh: head: 4 (over z), query: 4 (over y, x), ctx: 2 (over core).
Axes of the slice: x: 2, y: 2, z: 4, core: 2. Of those that a mesh axis runs over, the one named last changes fastest.
Arguments:
- queries: bfloat16 [1024, 128, 576], P('query', 'head'), may hold values from -3 to 3, as said below
- latent: bfloat16 [4096, 576], P(('head', 'query', 'ctx')), may hold values from -8 to 8
- out_grad: bfloat16 [1024, 128, 512], P('query', 'head'), may hold values from -6 to 6
- log_norms: float32 [1024, 128], P('query', 'head'), as said below
- row_dots: float32 [1024, 128], P('query', 'head'), may hold values from -48 to 48
Outputs:
- query_grad: float32 [1024, 128, 576], P(('query', 'ctx'), 'head')
- latent_grad: float32 [4096, 576], P(('head', 'query', 'ctx'))
The draws below stay inside these ranges and needn't reach their ends.
Inputs may be any that keep to these rules, and one draw needn't show every extreme that they name: queries and latent are of order one; latent rows may differ in scale. log_norms[i,h] is the log of the sum over all 4096 latent rows of exp(scores[i,h,j]), computed from the given queries and latent.
All inputs are finite; a program needn't handle non-finite values.
Results may differ from the reference program's by a relative error of at most 0.0029.
Values may be sent and summed in bfloat16 or wider, within the bound.
A program may use at most 128 MiB of HBM per device.

```python
import math
import jax
import jax.numpy as jnp
from jax import lax

H = 128
DV = 512
DK = 576
Q = 1024
L = 4096


softmax_scale = 192.0 ** (-0.5) * (0.1 * math.log(40.0) + 1.0) ** 2


def shared_fields(key):
    query_key = jax.random.fold_in(key, 11)
    latent_key = jax.random.fold_in(key, 23)
    queries = jnp.clip(0.5 * jax.random.normal(query_key, (Q, H, DK), jnp.float32), -3.0, 3.0)
    latent = jnp.clip(jax.random.normal(latent_key, (L, DK), jnp.float32), -4.0, 4.0)
    return (queries.astype(jnp.bfloat16), latent.astype(jnp.bfloat16))


def draw_queries(key, part):
    return shared_fields(key)[0]


def draw_latent(key, part):
    return shared_fields(key)[1]


def draw_log_norms(key, part):
    queries, latent = shared_fields(key)
    flat_q = queries.reshape(Q * H, DK)
    row_block = min(4096, Q * H)

    def per_block(block_rows):
        scores = lax.dot_general(block_rows, latent, (((1,), (1,)), ((), ())), preferred_element_type=jnp.float32) * softmax_scale
        highest = jnp.max(scores, axis=1, keepdims=True)
        return (highest + jnp.log(jnp.sum(jnp.exp(scores - highest), axis=1, keepdims=True)))[:, 0]
    blocks_all = flat_q.reshape(Q * H // row_block, row_block, DK)
    return lax.map(per_block, blocks_all).reshape(Q, H).astype(jnp.float32)


def block_levels(rng, dims, split, low, largest):
    gain = 1.0
    for position, shards_of in split:
        heights = jax.random.uniform(jax.random.fold_in(jax.random.fold_in(rng, 6), position), (shards_of,), jnp.float32, low / len(split), largest / len(split))
        gain = gain * jnp.repeat(jnp.exp(heights), dims[position] // shards_of).reshape((-1,) + (1,) * (len(dims) - 1 - position))
    return gain


def gaussian(key, extent, width, bound, cuts=(), held_as=jnp.bfloat16):
    loudness = block_levels(key, extent, cuts, -0.22, 0.18) if cuts else 1.0
    array = jax.random.normal(key, extent, jnp.float32) * width * loudness
    return jnp.minimum(jnp.maximum(array, -bound), bound).astype(held_as)


def setup_inputs(seed: int = 0) -> dict:
    key_of = jax.random.split(jax.random.key(seed), 6)
    return {
        "queries": draw_queries(jax.random.fold_in(key_of[5], 71), 0),
        "latent": draw_latent(jax.random.fold_in(key_of[5], 71), 0),
        "out_grad": gaussian(key_of[2], (Q, H, DV), 1.0, 6.0, ((0, 4), (1, 4))),
        "log_norms": draw_log_norms(jax.random.fold_in(key_of[5], 71), 0),
        "row_dots": gaussian(key_of[4], (Q, H), 8.0, 48.0, ((0, 4), (1, 4)), jnp.float32),
    }


softmax_scale = 192.0 ** -0.5 * (0.1 * math.log(40.0) + 1.0) ** 2


def reference(queries, latent, out_grad, log_norms, row_dots):
    head_group = 8
    group_count = H // head_group
    value_latent = latent[:, :DV]

    def per_group(index):
        first = index * head_group
        group_q = lax.dynamic_slice_in_dim(queries, first, head_group, 1).reshape(Q * head_group, DK)
        group_dout = lax.dynamic_slice_in_dim(out_grad, first, head_group, 1).reshape(Q * head_group, DV)
        norms = lax.dynamic_slice_in_dim(log_norms, first, head_group, 1).reshape(Q * head_group)
        dots = lax.dynamic_slice_in_dim(row_dots, first, head_group, 1).reshape(Q * head_group)
        scores = lax.dot_general(group_q, latent, (((1,), (1,)), ((), ())), preferred_element_type=jnp.float32) * softmax_scale
        probs = jnp.exp(scores - norms[:, None])
        probs_low = probs.astype(jnp.bfloat16)
        dprobs = lax.dot_general(group_dout, value_latent, (((1,), (1,)), ((), ())), preferred_element_type=jnp.float32)
        dscores = (probs * (dprobs - dots[:, None])).astype(jnp.bfloat16)
        query_part = jnp.dot(dscores, latent, preferred_element_type=jnp.float32) * softmax_scale
        latent_key = lax.dot_general(dscores, group_q, (((0,), (0,)), ((), ())), preferred_element_type=jnp.float32) * softmax_scale
        latent_value = lax.dot_general(probs_low, group_dout, (((0,), (0,)), ((), ())), preferred_element_type=jnp.float32)
        latent_part = latent_key + jnp.pad(latent_value, ((0, 0), (0, DK - DV)))
        return query_part.reshape(Q, head_group, DK), latent_part

    query_parts, latent_parts = lax.map(per_group, jnp.arange(group_count, dtype=jnp.int32))
    query_grad = jnp.transpose(query_parts, (1, 0, 2, 3)).reshape(Q, H, DK)
    latent_grad = jnp.sum(latent_parts, axis=0)
    return query_grad, latent_grad
```

```python
import functools
import math

import jax
import jax.numpy as jnp
from jax import lax
from jax.experimental import pallas as pl
from jax.experimental.pallas import tpu as pltpu
from jax.sharding import PartitionSpec as P

softmax_scale = 192.0 ** (-0.5) * (0.1 * math.log(40.0) + 1.0) ** 2
LOG2E = math.log2(math.e)
TILE_ROWS = 512
TILES = 2
SUM_TYPE = jnp.bfloat16

TRANS_B = (((1,), (1,)), ((), ()))
PLAIN = (((1,), (0,)), ((), ()))


def mm(a, b, dims=PLAIN):
    return lax.dot_general(a, b, dims, preferred_element_type=jnp.float32)


def side_by_side(parts):
    return parts[0] if len(parts) == 1 else jnp.concatenate(parts, axis=1)


def grads_kernel(tile_heads, has_init, is_last, *refs):
    refs = list(refs)
    q_ref, do_ref, norm_ref, dot_ref, lat_ref, latt_ref = refs[:6]
    init_ref = refs[6] if has_init else None
    *dq_refs, dl_ref, key, value = refs[6 + has_init :]
    heads, key_width, queries = q_ref.shape
    value_width = do_ref.shape[2]
    step = pl.program_id(0)
    upper = lax.axis_index("ctx") == 1

    @pl.when(step == 0)
    def _():
        key[...] = jnp.zeros_like(key)
        value[...] = jnp.zeros_like(value)

    def first(t):
        span = range(t * tile_heads, (t + 1) * tile_heads)
        q = side_by_side([q_ref[h] for h in span])
        do = do_ref[t * tile_heads : (t + 1) * tile_heads].reshape(tile_heads * queries, value_width)
        norms = side_by_side([norm_ref[h] for h in span]) * LOG2E
        dots = side_by_side([dot_ref[h] for h in span])
        s = mm(lat_ref[...], q)
        dp = mm(lat_ref[:, :value_width], do, TRANS_B)
        p = jnp.exp2(s * (softmax_scale * LOG2E) - norms)
        ds = (p * (dp - dots)).astype(jnp.bfloat16)
        return q, do, p.astype(jnp.bfloat16), ds

    def second(t, q, do, p, ds):
        part = mm(latt_ref[...], ds)
        for j in range(tile_heads):
            h = t * tile_heads + j
            piece = part[:, j * queries : (j + 1) * queries]
            if has_init:
                piece = piece + init_ref[h]
            if is_last:
                kept_ref, sent_ref = dq_refs
                half = queries // 2
                low, high = piece[:, :half] * softmax_scale, piece[:, half:] * softmax_scale
                kept_ref[h] = jnp.where(upper, high, low)
                sent_ref[h] = jnp.where(upper, low, high).astype(sent_ref.dtype)
            else:
                dq_refs[0][h] = piece
        key[...] += mm(q, ds, TRANS_B)
        value[...] += mm(p, do)

    count = heads // tile_heads
    held = first(0)
    for t in range(count):
        later = first(t + 1) if t + 1 < count else None
        second(t, *held)
        held = later

    @pl.when(step == pl.num_programs(0) - 1)
    def _():
        turned = key[...].T * softmax_scale
        dl_ref[:, :value_width] = (turned[:, :value_width] + value[...]).astype(dl_ref.dtype)
        dl_ref[:, value_width:] = turned[:, value_width:].astype(dl_ref.dtype)


def grads(q_t, do, norms, dots, lat, latt, init, sum_type, is_last):
    heads_all, key_width, queries = q_t.shape
    value_width = do.shape[2]
    ctx_rows = lat.shape[0]
    tile_heads = math.gcd(max(TILE_ROWS // queries, 1), heads_all)
    heads = math.gcd(tile_heads * TILES, heads_all)

    def by_head(i):
        return (i, 0, 0)

    def whole(i):
        return (0, 0)

    once = pl.Buffered(1)
    in_specs = [
        pl.BlockSpec((heads, key_width, queries), by_head),
        pl.BlockSpec((heads, queries, value_width), by_head),
        pl.BlockSpec((heads, 1, queries), by_head),
        pl.BlockSpec((heads, 1, queries), by_head),
        pl.BlockSpec((ctx_rows, key_width), whole, pipeline_mode=once),
        pl.BlockSpec((key_width, ctx_rows), whole, pipeline_mode=once),
    ]
    operands = [q_t, do, norms, dots, lat, latt]
    aliases = {}
    if init is not None:
        in_specs.append(pl.BlockSpec((heads, key_width, queries), by_head))
        operands.append(init)
        aliases = {} if is_last else {6: 0}
    grad_types = [(queries, jnp.float32)]
    if is_last:
        grad_types = [(queries // 2, jnp.float32), (queries // 2, jnp.bfloat16)]
    return pl.pallas_call(
        functools.partial(grads_kernel, tile_heads, init is not None, is_last),
        grid=(heads_all // heads,),
        in_specs=in_specs,
        out_specs=[
            *[pl.BlockSpec((heads, key_width, width), by_head) for width, _ in grad_types],
            pl.BlockSpec((ctx_rows, key_width), whole, pipeline_mode=once),
        ],
        scratch_shapes=[
            pltpu.VMEM((key_width, ctx_rows), jnp.float32),
            pltpu.VMEM((ctx_rows, value_width), jnp.float32),
        ],
        out_shape=[
            *[jax.ShapeDtypeStruct((heads_all, key_width, width), t) for width, t in grad_types],
            jax.ShapeDtypeStruct((ctx_rows, key_width), sum_type),
        ],
        input_output_aliases=aliases,
        compiler_params=pltpu.CompilerParams(vmem_limit_bytes=60 * 1024 * 1024),
    )(*operands)


def swap(x, axis, d):
    n = lax.axis_size(axis)
    assert n & (n - 1) == 0
    pairs = [(i, i ^ d) for i in range(n)]
    return lax.ppermute(x, axis, pairs)


def on_device(queries, latent, out_grad, log_norms, row_dots):
    local_queries, local_heads, key_width = queries.shape
    shard_rows = latent.shape[0]
    groups_head = lax.axis_size("head")
    groups_query = lax.axis_size("query")
    q_t = queries.transpose(1, 2, 0)
    do = out_grad.transpose(1, 0, 2)
    norms = log_norms.T.reshape(local_heads, 1, local_queries)
    dots = row_dots.T.reshape(local_heads, 1, local_queries)

    shards = [latent] + [swap(latent, "head", e) for e in range(1, groups_head)]
    shards, do = lax.optimization_barrier((shards, do))
    lat_own = jnp.concatenate(shards, axis=0)
    lats = [lat_own] + [swap(lat_own, "query", d) for d in range(1, groups_query)]
    query_sum = None
    terms = []
    order = [0] + list(range(groups_query - 1, 0, -1))
    for d in order:
        sum_type = SUM_TYPE if d else jnp.float32
        is_last = d == order[-1]
        *query_sum, part = grads(
            q_t, do, norms, dots, lats[d], lats[d].T, query_sum, sum_type, is_last
        )
        query_sum = query_sum if is_last else query_sum[0]
        terms.append(swap(part, "query", d) if d else part)
    kept, sent = query_sum
    received = swap(sent, "ctx", 1)
    total = sum((t.astype(jnp.float32) for t in terms[1:]), terms[0])
    blocks = [
        swap(total[e * shard_rows : (e + 1) * shard_rows].astype(SUM_TYPE), "head", e)
        for e in range(1, groups_head)
    ]
    query_grad = (kept + received.astype(jnp.float32)).transpose(2, 0, 1)
    blocks, query_grad = lax.optimization_barrier((blocks, query_grad))
    latent_grad = total[:shard_rows]
    for block in blocks:
        latent_grad = latent_grad + block.astype(jnp.float32)
    return (query_grad, latent_grad)


def solution(mesh):
    in_specs = (
        P("query", "head", None),
        P(("head", "query", "ctx"), None),
        P("query", "head", None),
        P("query", "head"),
        P("query", "head"),
    )
    out_specs = (P(("query", "ctx"), "head", None), P(("head", "query", "ctx"), None))
    return jax.shard_map(
        on_device, mesh=mesh, in_specs=in_specs, out_specs=out_specs, check_vma=False
    )
```
